32 devices in a mesh: shard: 2 (over x), ctx: 4 (over y, core), tp: 4 (over z).
Axes of the slice: x: 2, y: 2, z: 4, core: 2. Of those that a mesh axis runs over, the one named last changes fastest.
Arguments:
- stream: float32 [2048, 768], P(('shard', 'ctx')), may hold values from -6 to 6
- cotangent: float32 [2048, 768], P(('shard', 'ctx')), may hold values from -6 to 6
- segments: int32 [2048], P(('shard', 'ctx')), may hold values from 0 to 2047, as said below
- positions: int32 [2048], P(('shard', 'ctx')), may hold values from 0 to 511, as said below
- norm_gains: bfloat16 [2, 2, 768], P(None, None, 'shard'), may hold values from 0.099609375 to 1.8984375
- norm_shifts: bfloat16 [2, 2, 768], P(None, None, 'shard'), may hold values from -3 to 3
- qkv_weight: bfloat16 [2, 768, 2304], P(None, 'shard', 'tp'), may hold values from -0.21875 to 0.21875
- qkv_bias: bfloat16 [2, 12, 192], P(None, 'tp', 'shard'), may hold values from -3 to 3
- out_weight: bfloat16 [2, 768, 768], P(None, 'tp', 'shard'), may hold values from -1.75 to 1.75
- up_weight: bfloat16 [2, 768, 3072], P(None, 'shard', 'tp'), may hold values from -0.21875 to 0.21875
- up_bias: bfloat16 [2, 24, 128], P(None, 'tp', 'shard'), may hold values from -3 to 3
- down_weight: bfloat16 [2, 3072, 768], P(None, 'tp', 'shard'), may hold values from -0.109375 to 0.109375
- out_biases: bfloat16 [2, 2, 768], P(None, None, 'shard'), may hold values from -3 to 3
Outputs:
- result_stream: float32 [2048, 768], P(('shard', 'ctx'))
- grad_stream: float32 [2048, 768], P(('shard', 'ctx'))
- grad_norm_gains: float32 [2, 2, 768], P(None, None, 'shard')
- grad_norm_shifts: float32 [2, 2, 768], P(None, None, 'shard')
- grad_qkv_weight: float32 [2, 768, 2304], P(None, 'shard', 'tp')
- grad_qkv_bias: float32 [2, 12, 192], P(None, 'tp', 'shard')
- grad_out_weight: float32 [2, 768, 768], P(None, 'tp', 'shard')
- grad_up_weight: float32 [2, 768, 3072], P(None, 'shard', 'tp')
- grad_up_bias: float32 [2, 24, 128], P(None, 'tp', 'shard')
- grad_down_weight: float32 [2, 3072, 768], P(None, 'tp', 'shard')
- grad_out_biases: float32 [2, 2, 768], P(None, None, 'shard')
The draws below stay inside these ranges and needn't reach their ends.
Inputs may be any that keep to these rules, and one draw needn't show every extreme that they name: `segments`: tokens with equal numbers form one sequence, which lies within one index of shard and has at most 512 tokens; numbers are not consecutive. Every index of shard holds one sequence of exactly 512 tokens, and the last token of every index of shard in packed order is a sequence of its own. The sequences of an index of shard are packed into blocks of 128 tokens, which are dealt to its devices along ctx, 2 a device, in a drawn order. `positions`: A token's place in its sequence, counted from 0 along the sequence.
All inputs are finite; a program needn't handle non-finite values.
Results may differ from the reference program's by a relative error of at most 0.04.
Values may be sent and summed in bfloat16 or wider, within the bound.
No kernel may reach another device: no remote copies, remote signals or barrier semaphores. Data moves between devices by JAX's collectives and lax.ppermute only.
A program may use at most 128 MiB of HBM per device.

```python
import math
import jax
import jax.numpy as jnp
from jax import lax

D = 768
HEADS = 12
HD = 64
ROT = 16
FF = 3072
LAYERS = 2
BLOCK = 128
SEQ_MAX = 512
GROUP_TOK = 1024
TOKENS = 2048


def packed_tokens(key):
    base_key = jax.random.fold_in(key, 7)
    coin_key = jax.random.fold_in(base_key, 1)
    deal_key = jax.random.fold_in(base_key, 2)
    places = jnp.arange(TOKENS, dtype=jnp.int32)
    within = places % GROUP_TOK
    coins = jax.random.randint(coin_key, (TOKENS,), 0, 160) == 0
    starts = (within % SEQ_MAX == 0) | (within >= SEQ_MAX) & coins | (within == GROUP_TOK - 1)
    latest = lax.cummax(jnp.where(starts, places, 0), axis=0).astype(jnp.int32)
    numbers = latest
    offsets = (places - latest).astype(jnp.int32)
    group_count = TOKENS // GROUP_TOK
    block_count = GROUP_TOK // BLOCK

    def deal_group(group_index):
        return jax.random.permutation(jax.random.fold_in(deal_key, group_index), block_count).astype(jnp.int32)
    orders = jax.vmap(deal_group)(jnp.arange(group_count, dtype=jnp.int32))
    picks = jnp.broadcast_to(orders[:, :, None], (group_count, block_count, BLOCK))
    dealt_numbers = jnp.take_along_axis(numbers.reshape(group_count, block_count, BLOCK), picks, axis=1)
    dealt_offsets = jnp.take_along_axis(offsets.reshape(group_count, block_count, BLOCK), picks, axis=1)
    return (dealt_numbers.reshape(TOKENS).astype(jnp.int32), dealt_offsets.reshape(TOKENS).astype(jnp.int32))


def draw_segments(key, part):
    return packed_tokens(key)[0]


def draw_positions(key, part):
    return packed_tokens(key)[1]


def block_scale(rng, shape, shards, least, largest):
    loudness, own = 1.0, jax.random.fold_in(rng, 6)
    for dim, blocks in shards:
        steps = jnp.exp(jax.random.uniform(jax.random.fold_in(own, dim), (blocks,), jnp.float32, least / len(shards), largest / len(shards)))
        loudness = loudness * jnp.repeat(steps, shape[dim] // blocks).reshape([-1 if axis == dim else 1 for axis in range(len(shape))])
    return loudness


def gaussian(key, shape, scale, limit, split=(), kind=jnp.bfloat16):
    entries = scale * jax.random.normal(key, shape, jnp.float32)
    if split:
        entries = entries * block_scale(key, shape, split, -0.22, 0.18)
    return jnp.clip(entries, -limit, limit).astype(kind)


def setup_inputs(seed: int = 0) -> dict:
    splits = jax.random.split(jax.random.key(seed), 14)
    return {
        "stream": gaussian(splits[0], (TOKENS, D), 1.0, 6.0, ((0, 8),), jnp.float32),
        "cotangent": gaussian(splits[1], (TOKENS, D), 1.0, 6.0, ((0, 8),), jnp.float32),
        "segments": draw_segments(jax.random.fold_in(splits[13], 71), 0),
        "positions": draw_positions(jax.random.fold_in(splits[13], 71), 0),
        "norm_gains": jnp.clip(1.0 + 0.18 * jax.random.normal(splits[4], (LAYERS, 2, D), jnp.float32), 0.099609375, 1.8984375).astype(jnp.bfloat16),
        "norm_shifts": gaussian(splits[5], (LAYERS, 2, D), 0.5, 3.0, ((2, 2),)),
        "qkv_weight": gaussian(splits[6], (LAYERS, D, 3 * D), D ** -0.5, 0.21875, ((1, 2), (2, 4))),
        "qkv_bias": gaussian(splits[7], (LAYERS, HEADS, 3 * HD), 0.5, 3.0, ((1, 4), (2, 2))),
        "out_weight": gaussian(splits[8], (LAYERS, D, D), (D // 64) ** -0.5, 1.75, ((1, 4), (2, 2))),
        "up_weight": gaussian(splits[9], (LAYERS, D, FF), D ** -0.5, 0.21875, ((1, 2), (2, 4))),
        "up_bias": gaussian(splits[10], (LAYERS, FF // 128, 128), 0.5, 3.0, ((1, 4), (2, 2))),
        "down_weight": gaussian(splits[11], (LAYERS, FF, D), FF ** -0.5, 0.109375, ((1, 4), (2, 2))),
        "out_biases": gaussian(splits[12], (LAYERS, 2, D), 0.5, 3.0, ((2, 2),)),
    }


EPSILON = 1e-05
SCORE_SCALE = 0.125
ROOT_HALF = 0.7071067811865476
INVERSE_ROOT_TWO_PI = 0.3989422804014327

def normalize(values_in):
    centre = lax.optimization_barrier(jnp.mean(values_in, axis=-1, keepdims=True))
    centered = values_in - centre
    spread = lax.optimization_barrier(jnp.mean(centered * centered, axis=-1, keepdims=True))
    inverse = lax.rsqrt(spread + EPSILON)
    return (centered * inverse, inverse)

def norm_backward(grad_out, normed, inverse, gain_row):
    scaled = grad_out * gain_row
    first_mean = lax.optimization_barrier(jnp.mean(scaled, axis=-1, keepdims=True))
    second = lax.optimization_barrier(jnp.mean(scaled * normed, axis=-1, keepdims=True))
    return (scaled - first_mean - normed * second) * inverse

def gelu_value(hidden):
    return 0.5 * hidden * (1.0 + jax.scipy.special.erf(hidden * ROOT_HALF))

def gelu_slope(hidden):
    cumulative = 0.5 * (1.0 + jax.scipy.special.erf(hidden * ROOT_HALF))
    return cumulative + hidden * jnp.exp(-0.5 * hidden * hidden) * INVERSE_ROOT_TWO_PI

def rotary_tables(token_places):
    halfway = ROT // 2
    inverse = jnp.exp(jnp.arange(halfway, dtype=jnp.float32) * (-math.log(10000.0) / halfway))
    angles = token_places.astype(jnp.float32)[:, None] * inverse[None, :]
    angles = jnp.concatenate([angles, angles], axis=-1)
    return (jnp.cos(angles), jnp.sin(angles))

def rotate(values_in, cosine, sine_table):
    halfway = ROT // 2
    leading = values_in[..., :ROT]
    turned = jnp.concatenate([-leading[..., halfway:], leading[..., :halfway]], axis=-1)
    mixed_part = leading * cosine[:, None, :] + turned * sine_table[:, None, :]
    return jnp.concatenate([mixed_part, values_in[..., ROT:]], axis=-1)

def unrotate(grads_in, cosine, sine_table):
    halfway = ROT // 2
    leading = grads_in[..., :ROT]
    weighted = leading * sine_table[:, None, :]
    returned = jnp.concatenate([weighted[..., halfway:], -weighted[..., :halfway]], axis=-1)
    return jnp.concatenate([leading * cosine[:, None, :] + returned, grads_in[..., ROT:]], axis=-1)

def swap_heads(array_in):
    return jnp.swapaxes(array_in, 0, 1)

def head_forward(query_head, keys_head, values_head, allowed):
    scores = jnp.dot(query_head, keys_head.T, preferred_element_type=jnp.float32) * SCORE_SCALE
    row_total = lax.optimization_barrier(jnp.sum(jnp.where(allowed, jnp.exp(scores), 0.0), axis=-1, keepdims=True))
    log_total = jnp.log(row_total)
    probabilities = jnp.where(allowed, jnp.exp(scores - log_total), 0.0).astype(jnp.bfloat16)
    attended = jnp.dot(probabilities, values_head, preferred_element_type=jnp.float32).astype(jnp.bfloat16)
    return (attended, log_total[:, 0])

def head_backward(query_head, keys_head, values_head, attended, log_total, grad_attended, allowed):
    scores = jnp.dot(query_head, keys_head.T, preferred_element_type=jnp.float32) * SCORE_SCALE
    exact = jnp.where(allowed, jnp.exp(scores - log_total[:, None]), 0.0)
    grad_values = jnp.dot(exact.astype(jnp.bfloat16).T, grad_attended, preferred_element_type=jnp.float32)
    grad_probs = jnp.dot(grad_attended, values_head.T, preferred_element_type=jnp.float32)
    offset = lax.optimization_barrier(jnp.sum(grad_attended.astype(jnp.float32) * attended.astype(jnp.float32), axis=-1, keepdims=True))
    grad_scores = (exact * (grad_probs - offset) * SCORE_SCALE).astype(jnp.bfloat16)
    grad_query = jnp.dot(grad_scores, keys_head, preferred_element_type=jnp.float32)
    grad_keys = jnp.dot(grad_scores.T, query_head, preferred_element_type=jnp.float32)
    return (grad_query, grad_keys, grad_values)

def layer_forward(stream_in, cosine, sine_table, allowed, params):
    gain_rows, shifts, qkv_full, qkv_flat, out_full, up_full, up_flat, down_full, bias_rows = params
    row_count = stream_in.shape[0]
    normed, inverse = normalize(stream_in)
    hidden_one = (normed * gain_rows[0] + shifts[0]).astype(jnp.bfloat16)
    hidden_two = (normed * gain_rows[1] + shifts[1]).astype(jnp.bfloat16)
    projected = jnp.dot(hidden_one, qkv_full, preferred_element_type=jnp.float32) + qkv_flat
    projected = projected.reshape(row_count, HEADS, 3 * HD)
    rotated_query = rotate(projected[..., :HD], cosine, sine_table).astype(jnp.bfloat16)
    rotated_keys = rotate(projected[..., HD:2 * HD], cosine, sine_table).astype(jnp.bfloat16)
    value_rows = projected[..., 2 * HD:].astype(jnp.bfloat16)

    def one_head(operands):
        return head_forward(operands[0], operands[1], operands[2], allowed)
    attended, log_total = lax.map(one_head, (swap_heads(rotated_query), swap_heads(rotated_keys), swap_heads(value_rows)))
    attended = swap_heads(attended)
    upward = jnp.dot(hidden_two, up_full, preferred_element_type=jnp.float32) + up_flat
    activated = gelu_value(upward).astype(jnp.bfloat16)
    mixed_sum = jnp.dot(attended.reshape(row_count, D), out_full, preferred_element_type=jnp.float32)
    mixed_sum = mixed_sum + jnp.dot(activated, down_full, preferred_element_type=jnp.float32)
    result = stream_in + mixed_sum + bias_rows[0] + bias_rows[1]
    stored = (normed, inverse, hidden_one, hidden_two, rotated_query, rotated_keys, value_rows, attended, log_total, upward, activated)
    return (result, stored)

def layer_backward(grad_result, cosine, sine_table, allowed, params, stored):
    gain_rows, shifts, qkv_full, qkv_flat, out_full, up_full, up_flat, down_full, bias_rows = params
    normed, inverse, hidden_one, hidden_two, rotated_query, rotated_keys, value_rows, attended, log_total, upward, activated = stored
    row_count = grad_result.shape[0]
    grad_low = grad_result.astype(jnp.bfloat16)
    grad_bias = lax.optimization_barrier(jnp.sum(grad_result, axis=0))
    grad_out_b = jnp.stack([grad_bias, grad_bias])
    grad_down = jnp.dot(activated.T, grad_low, preferred_element_type=jnp.float32)
    grad_act = jnp.dot(grad_low, down_full.T, preferred_element_type=jnp.float32)
    grad_upward = (grad_act * gelu_slope(upward)).astype(jnp.bfloat16)
    grad_up_b = lax.optimization_barrier(jnp.sum(grad_upward.astype(jnp.float32), axis=0))
    grad_up = jnp.dot(hidden_two.T, grad_upward, preferred_element_type=jnp.float32)
    grad_two = jnp.dot(grad_upward, up_full.T, preferred_element_type=jnp.float32)
    grad_out = jnp.dot(attended.reshape(row_count, D).T, grad_low, preferred_element_type=jnp.float32)
    grad_attended = jnp.dot(grad_low, out_full.T, preferred_element_type=jnp.float32).astype(jnp.bfloat16)
    grad_attended = grad_attended.reshape(row_count, HEADS, HD)

    def one_head(operands):
        return head_backward(operands[0], operands[1], operands[2], operands[3], operands[4], operands[5], allowed)
    grad_query, grad_keys, grad_values = lax.map(one_head, (swap_heads(rotated_query), swap_heads(rotated_keys), swap_heads(value_rows), swap_heads(attended), log_total, swap_heads(grad_attended)))
    grad_query = unrotate(swap_heads(grad_query), cosine, sine_table)
    grad_keys = unrotate(swap_heads(grad_keys), cosine, sine_table)
    grad_projected = jnp.concatenate([grad_query, grad_keys, swap_heads(grad_values)], axis=-1).astype(jnp.bfloat16)
    grad_projected = grad_projected.reshape(row_count, 3 * D)
    grad_qkv_b = lax.optimization_barrier(jnp.sum(grad_projected.astype(jnp.float32), axis=0))
    grad_qkv = jnp.dot(hidden_one.T, grad_projected, preferred_element_type=jnp.float32)
    grad_one = jnp.dot(grad_projected, qkv_full.T, preferred_element_type=jnp.float32)
    grad_gains = jnp.stack([lax.optimization_barrier(jnp.sum(grad_one * normed, axis=0)), lax.optimization_barrier(jnp.sum(grad_two * normed, axis=0))])
    grad_shifts = jnp.stack([lax.optimization_barrier(jnp.sum(grad_one, axis=0)), lax.optimization_barrier(jnp.sum(grad_two, axis=0))])
    grad_stream = grad_result + norm_backward(grad_one, normed, inverse, gain_rows[0]) + norm_backward(grad_two, normed, inverse, gain_rows[1])
    grads = (grad_gains, grad_shifts, grad_qkv, grad_qkv_b, grad_out, grad_up, grad_up_b, grad_down, grad_out_b)
    return (grad_stream, grads)

def layer_params(layer_index, norm_gains, norm_shifts, qkv_weight, qkv_bias, out_weight, up_weight, up_bias, down_weight, out_biases):
    return (norm_gains[layer_index].astype(jnp.float32), norm_shifts[layer_index].astype(jnp.float32), qkv_weight[layer_index], qkv_bias[layer_index].astype(jnp.float32).reshape(3 * D), out_weight[layer_index], up_weight[layer_index], up_bias[layer_index].astype(jnp.float32).reshape(FF), down_weight[layer_index], out_biases[layer_index].astype(jnp.float32))

def accumulate(total_grad, new_grad):
    return total_grad + new_grad

def reference(stream, cotangent, segments, positions, norm_gains, norm_shifts, qkv_weight, qkv_bias, out_weight, up_weight, up_bias, down_weight, out_biases):
    params = [layer_params(layer_index, norm_gains, norm_shifts, qkv_weight, qkv_bias, out_weight, up_weight, up_bias, down_weight, out_biases) for layer_index in range(LAYERS)]
    groups = TOKENS // GROUP_TOK

    def one_group(running, operands):
        group_stream, group_cotangent, group_segments, group_places = operands
        cosine, sine_table = rotary_tables(group_places)
        allowed = (group_segments[:, None] == group_segments[None, :]) & (group_places[None, :] <= group_places[:, None])
        current = group_stream
        stored_layers = []
        for layer_index in range(LAYERS):
            current, stored = layer_forward(current, cosine, sine_table, allowed, params[layer_index])
            stored_layers.append(stored)
        grad_current = group_cotangent
        updated = list(running)
        for layer_index in reversed(range(LAYERS)):
            grad_current, grads = layer_backward(grad_current, cosine, sine_table, allowed, params[layer_index], stored_layers[layer_index])
            updated[layer_index] = jax.tree.map(accumulate, running[layer_index], grads)
        return (tuple(updated), (current, grad_current))
    zero_grads = tuple(((jnp.zeros((2, D), jnp.float32), jnp.zeros((2, D), jnp.float32), jnp.zeros((D, 3 * D), jnp.float32), jnp.zeros((3 * D,), jnp.float32), jnp.zeros((D, D), jnp.float32), jnp.zeros((D, FF), jnp.float32), jnp.zeros((FF,), jnp.float32), jnp.zeros((FF, D), jnp.float32), jnp.zeros((2, D), jnp.float32)) for layer_index in range(LAYERS)))
    operands = (stream.reshape(groups, GROUP_TOK, D), cotangent.reshape(groups, GROUP_TOK, D), segments.reshape(groups, GROUP_TOK), positions.reshape(groups, GROUP_TOK))
    totals, (results, grad_inputs) = lax.scan(one_group, zero_grads, operands)

    def stacked(member):
        return jnp.stack([totals[layer_index][member] for layer_index in range(LAYERS)])
    return (results.reshape(TOKENS, D), grad_inputs.reshape(TOKENS, D), stacked(0), stacked(1), stacked(2), stacked(3).reshape(LAYERS, HEADS, 3 * HD), stacked(4), stacked(5), stacked(6).reshape(LAYERS, FF // 128, 128), stacked(7), stacked(8))
```

```python
import math

import jax
import jax.numpy as jnp
from jax import lax
from jax.sharding import PartitionSpec as P

HD = 64
ROT = 16
LAYERS = 2
EPSILON = 1e-05
SCORE_SCALE = 0.125
ROOT_HALF = 0.7071067811865476
INVERSE_ROOT_TWO_PI = 0.3989422804014327
BF = jnp.bfloat16
F32 = jnp.float32


def bits_of(count):
    return [1 << place for place in range(count.bit_length() - 1)]


def dot(left, right):
    return jnp.dot(left, right, preferred_element_type=F32)


def dot_nt(left, right):
    return lax.dot_general(left, right, (((1,), (1,)), ((), ())), preferred_element_type=F32)


def dot_tn(left, right):
    return lax.dot_general(left, right, (((0,), (0,)), ((), ())), preferred_element_type=F32)


def normalize(values_in):
    centre = jnp.mean(values_in, axis=-1, keepdims=True)
    centered = values_in - centre
    spread = jnp.mean(centered * centered, axis=-1, keepdims=True)
    inverse = lax.rsqrt(spread + EPSILON)
    return (centered * inverse, inverse)


def gelu_both(hidden):
    cumulative = 0.5 * (1.0 + lax.erf(hidden * ROOT_HALF))
    slope = cumulative + hidden * jnp.exp(-0.5 * hidden * hidden) * INVERSE_ROOT_TWO_PI
    return hidden * cumulative, slope


def rotary_tables(token_places):
    halfway = ROT // 2
    inverse = jnp.exp(jnp.arange(halfway, dtype=F32) * (-math.log(10000.0) / halfway))
    angles = token_places.astype(F32)[:, None] * inverse[None, :]
    angles = jnp.concatenate([angles, angles], axis=-1)
    return (jnp.cos(angles), jnp.sin(angles))


def rotate(values_in, cosine, sine_table):
    halfway = ROT // 2
    leading = values_in[..., :ROT]
    turned = jnp.concatenate([-leading[..., halfway:], leading[..., :halfway]], axis=-1)
    mixed_part = leading * cosine[:, None, :] + turned * sine_table[:, None, :]
    return jnp.concatenate([mixed_part, values_in[..., ROT:]], axis=-1)


def unrotate(grads_in, cosine, sine_table):
    halfway = ROT // 2
    leading = grads_in[..., :ROT]
    weighted = leading * sine_table[:, None, :]
    returned = jnp.concatenate([weighted[..., halfway:], -weighted[..., :halfway]], axis=-1)
    return jnp.concatenate([leading * cosine[:, None, :] + returned, grads_in[..., ROT:]], axis=-1)


def make_shards(sizes):
    n_shard, n_ctx, n_tp = sizes["shard"], sizes["ctx"], sizes["tp"]
    core_bits, far_bits = bits_of(n_ctx)[:1], bits_of(n_ctx)[1:]
    n_half = 2 if core_bits else 1

    def swap(value, axis, bit):
        return lax.ppermute(value, axis, [(i, i ^ bit) for i in range(sizes[axis])])

    def gather_shard(value, dim=0):
        for bit in bits_of(n_shard):
            value = jnp.concatenate([value, swap(value, "shard", bit)], axis=dim)
        return value

    def gather_core(value, dim=0):
        for bit in core_bits:
            value = jnp.concatenate([value, swap(value, "ctx", bit)], axis=dim)
        return value

    def gather_ctx(value):
        for bit in far_bits + core_bits:
            value = jnp.concatenate([value, swap(value, "ctx", bit)], axis=0)
        return value

    def halve(value, axis, bit):
        half = value.shape[0] // 2
        received = swap(value[half:].astype(BF), axis, bit)
        return value[:half].astype(F32) + received.astype(F32)

    def scatter_ctx(value):
        for bit in reversed(far_bits + core_bits):
            value = halve(value, "ctx", bit)
        return value

    def reduce_tp(partial):
        partial = partial.astype(BF)
        rest = bits_of(n_tp)
        if not rest:
            return partial
        value = halve(partial, "tp", rest[0]).astype(BF)
        for bit in rest[1:]:
            value = (value.astype(F32) + swap(value, "tp", bit).astype(F32)).astype(BF)
        return jnp.concatenate([value, swap(value, "tp", rest[0])], axis=0)

    def reduce_weight(grad):
        for bit in core_bits:
            grad = halve(grad, "ctx", bit)
        for bit in reversed(bits_of(n_shard)):
            grad = halve(grad, "shard", bit)
        grad = grad.astype(BF)
        for bit in far_bits:
            grad = (grad.astype(F32) + swap(grad, "ctx", bit).astype(F32)).astype(BF)
        for bit in core_bits:
            other = swap(grad, "ctx", bit)
            odd = (lax.axis_index("ctx") & bit) != 0
            grad = jnp.where(
                odd, jnp.concatenate([other, grad], 0), jnp.concatenate([grad, other], 0)
            )
        return grad.astype(F32)

    def reduce_small(value):
        for axis, axis_bits in (
            ("ctx", bits_of(n_ctx)),
            ("shard", bits_of(n_shard)),
            ("tp", bits_of(n_tp)),
        ):
            for bit in axis_bits:
                value = value + swap(value, axis, bit)
        return value

    def flip_if(value, dim, bit, condition):
        order = [i ^ bit for i in range(value.shape[dim])]
        pieces = [lax.index_in_dim(value, i, dim, keepdims=True) for i in order]
        return jnp.where(condition, jnp.concatenate(pieces, axis=dim), value)

    def reorder(value, index_shard, index_core):
        dim = value.ndim
        for bit in bits_of(n_shard):
            value = flip_if(value, dim - 3, bit, (index_shard & bit) != 0)
        for bit in core_bits:
            value = flip_if(value, dim - 2, bit, (index_core & bit) != 0)
        return value

    def shards(
        stream,
        cotangent,
        segments,
        positions,
        norm_gains,
        norm_shifts,
        qkv_weight,
        qkv_bias,
        out_weight,
        up_weight,
        up_bias,
        down_weight,
        out_biases,
    ):
        rows, width = stream.shape
        own = width // n_shard
        piece = own // n_half
        heads = qkv_bias.shape[1]
        s, c, t = lax.axis_index("shard"), lax.axis_index("ctx"), lax.axis_index("tp")
        core = (c & 1) if core_bits else jnp.int32(0)
        odd_tp = (t & 1) != 0

        def swap_rows(value):
            if n_tp == 1:
                return value
            half = value.shape[0] // 2
            return jnp.where(odd_tp, jnp.concatenate([value[half:], value[:half]], 0), value)

        def enter(value):
            value = reorder(value.reshape(rows, n_shard, n_half, piece), s, core)
            return swap_rows(jnp.swapaxes(value, 1, 2).reshape(rows, width))

        def leave(value):
            value = swap_rows(value)
            value = jnp.swapaxes(value.reshape(rows, n_half, n_shard, piece), 1, 2)
            return reorder(value, s, core).reshape(rows, width)

        def vec_piece(value):
            return lax.dynamic_slice_in_dim(value, core * piece, piece, axis=value.ndim - 1)

        small = jnp.concatenate(
            [
                norm_gains.reshape(-1, own),
                norm_shifts.reshape(-1, own),
                out_biases.reshape(-1, own),
            ],
            0,
        )
        small = gather_core(gather_shard(vec_piece(small), 1), 1).astype(F32)
        gains = small[: 2 * LAYERS].reshape(LAYERS, 2, width)
        shifts = small[2 * LAYERS : 4 * LAYERS].reshape(LAYERS, 2, width)
        biases = small[4 * LAYERS :].reshape(LAYERS, 2, width)
        flat = jnp.concatenate([qkv_bias.reshape(1, -1), up_bias.reshape(1, -1)], 1)
        flat = gather_shard(flat, 0)
        for bit in bits_of(n_shard):
            flat = flip_if(flat, 0, bit, (s & bit) != 0)
        cut = qkv_bias.size
        qkv_flat = jnp.moveaxis(flat[:, :cut].reshape((n_shard,) + qkv_bias.shape), 0, 2)
        qkv_flat = qkv_flat.reshape(LAYERS, -1).astype(F32)
        up_flat = jnp.moveaxis(flat[:, cut:].reshape((n_shard,) + up_bias.shape), 0, 2)
        up_flat = up_flat.reshape(LAYERS, -1).astype(F32)
        qkv_width, up_width, out_width = qkv_weight.shape[2], up_weight.shape[2], out_weight.shape[1]

        def rows_piece(value):
            return lax.dynamic_slice_in_dim(value, core * piece, piece, axis=0)

        def fetch(layer):
            first = gather_core(gather_shard(rows_piece(qkv_weight[layer])))
            later = jnp.concatenate(
                [
                    rows_piece(up_weight[layer]),
                    vec_piece(out_weight[layer]).T,
                    vec_piece(down_weight[layer]).T,
                ],
                1,
            )
            later = gather_core(gather_shard(later))
            return first, later

        weights = [fetch(layer) for layer in range(LAYERS)]

        stream_in = enter(stream)
        grad_in = enter(cotangent)
        marks = swap_rows(jnp.stack([segments, positions], 1))
        places = marks[:, 1]
        all_marks = gather_ctx(marks)
        allowed = (marks[:, None, 0] == all_marks[None, :, 0]) & (
            all_marks[None, :, 1] <= marks[:, None, 1]
        )
        head_mask = allowed[None]
        cosine, sine_table = rotary_tables(places)

        def forward(stream_now, layer):
            first, later = weights[layer]
            up_full = later[:, :up_width]
            mix_full = later[:, up_width:]
            normed, inverse = normalize(stream_now)
            hidden_one = (normed * gains[layer, 0] + shifts[layer, 0]).astype(BF)
            hidden_two = (normed * gains[layer, 1] + shifts[layer, 1]).astype(BF)
            projected = (dot(hidden_one, first) + qkv_flat[layer]).reshape(rows, heads, 3 * HD)
            query = rotate(projected[..., :HD], cosine, sine_table).astype(BF)
            keys = rotate(projected[..., HD : 2 * HD], cosine, sine_table).astype(BF)
            values = projected[..., 2 * HD :].astype(BF)
            pairs = jnp.concatenate([keys.reshape(rows, -1), values.reshape(rows, -1)], -1)
            pairs = gather_ctx(pairs)
            all_keys = pairs[:, : heads * HD].reshape(-1, heads, HD)
            all_values = pairs[:, heads * HD :].reshape(-1, heads, HD)
            upward = dot(hidden_two, up_full) + up_flat[layer]
            activated, slope = gelu_both(upward)
            activated = activated.astype(BF)
            scores = (
                jnp.einsum("qhd,khd->hqk", query, all_keys, preferred_element_type=F32)
                * SCORE_SCALE
            )
            row_total = jnp.sum(jnp.where(head_mask, jnp.exp(scores), 0.0), -1, keepdims=True)
            log_total = jnp.log(row_total)
            probs = jnp.where(head_mask, jnp.exp(scores - log_total), 0.0).astype(BF)
            attended = jnp.einsum(
                "hqk,khd->qhd", probs, all_values, preferred_element_type=F32
            ).astype(BF)
            mixed = jnp.concatenate([attended.reshape(rows, -1), activated], 1)
            total = reduce_tp(dot_nt(mixed, mix_full))
            result = stream_now + total.astype(F32) + biases[layer, 0] + biases[layer, 1]
            stored = (
                normed, inverse, hidden_one, hidden_two, query, all_keys, all_values,
                attended, log_total, mixed, slope,
            )
            return result, stored

        def backward(grad_result, layer, stored):
            first, later = weights[layer]
            (
                normed, inverse, hidden_one, hidden_two, query, all_keys, all_values,
                attended, log_total, mixed, slope,
            ) = stored
            grad_low = grad_result.astype(BF)
            grad_bias = jnp.sum(grad_result, axis=0)
            grad_act = dot(grad_low, later[:, up_width + out_width :])
            grad_upward = (grad_act * slope).astype(BF)
            grad_up_b = jnp.sum(grad_upward.astype(F32), axis=0)
            grad_two = dot_nt(grad_upward, later[:, :up_width])
            grad_rest = jnp.concatenate(
                [dot_tn(hidden_two, grad_upward).astype(BF), dot_tn(grad_low, mixed).astype(BF)], 1
            )
            reduced_rest = reduce_weight(grad_rest)
            grad_att = dot(grad_low, later[:, up_width : up_width + out_width]).astype(BF)
            grad_att = grad_att.reshape(rows, heads, HD)
            scores = (
                jnp.einsum("qhd,khd->hqk", query, all_keys, preferred_element_type=F32)
                * SCORE_SCALE
            )
            exact = jnp.where(head_mask, jnp.exp(scores - log_total), 0.0)
            grad_probs = jnp.einsum(
                "qhd,khd->hqk", grad_att, all_values, preferred_element_type=F32
            )
            offset = jnp.sum(grad_att.astype(F32) * attended.astype(F32), axis=-1)
            grad_scores = (exact * (grad_probs - offset.T[:, :, None]) * SCORE_SCALE).astype(BF)
            grad_query = jnp.einsum(
                "hqk,khd->qhd", grad_scores, all_keys, preferred_element_type=F32
            )
            grad_values = jnp.einsum(
                "hqk,qhd->khd", exact.astype(BF), grad_att, preferred_element_type=F32
            )
            grad_keys = jnp.einsum(
                "hqk,qhd->khd", grad_scores, query, preferred_element_type=F32
            )
            total_keys = all_keys.shape[0]
            pair_grads = jnp.concatenate(
                [grad_keys.reshape(total_keys, -1), grad_values.reshape(total_keys, -1)], -1
            ).astype(BF)
            own_grads = scatter_ctx(pair_grads)
            grad_keys = own_grads[:, : heads * HD].reshape(rows, heads, HD)
            grad_values = own_grads[:, heads * HD :].reshape(rows, heads, HD)
            grad_projected = jnp.concatenate(
                [
                    unrotate(grad_query, cosine, sine_table),
                    unrotate(grad_keys, cosine, sine_table),
                    grad_values,
                ],
                axis=-1,
            ).astype(BF)
            grad_projected = grad_projected.reshape(rows, -1)
            grad_qkv_b = jnp.sum(grad_projected.astype(F32), axis=0)
            reduced_qkv = reduce_weight(dot_tn(hidden_one, grad_projected).astype(BF))
            grad_one = dot_nt(grad_projected, first)
            vectors = jnp.concatenate(
                [
                    jnp.sum(grad_one * normed, axis=0),
                    jnp.sum(grad_two * normed, axis=0),
                    jnp.sum(grad_one, axis=0),
                    jnp.sum(grad_two, axis=0),
                ]
            )
            scaled = grad_one * gains[layer, 0] + grad_two * gains[layer, 1]
            scaled = reduce_tp(scaled).astype(F32)
            first_mean = jnp.mean(scaled, axis=-1, keepdims=True)
            second = jnp.mean(scaled * normed, axis=-1, keepdims=True)
            grad_stream = grad_result + (scaled - first_mean - normed * second) * inverse
            return grad_stream, (reduced_qkv, reduced_rest, vectors, grad_bias, grad_qkv_b, grad_up_b)

        current, kept = stream_in, []
        for layer in range(LAYERS):
            current, stored = forward(current, layer)
            kept.append(stored)
        grad_current, grads = grad_in, [None] * LAYERS
        for layer in reversed(range(LAYERS)):
            grad_current, grads[layer] = backward(grad_current, layer, kept[layer])

        first_tp = (t == 0).astype(F32)
        tp_vectors = jnp.concatenate([g[2] for g in grads] + [g[3] * first_tp for g in grads])
        vector_rows = tp_vectors.reshape(-1, n_half, n_shard, piece)
        vector_rows = reorder(jnp.swapaxes(vector_rows, 1, 2), s, core).reshape(-1, width)
        bias_rows = jnp.concatenate([g[4] for g in grads] + [g[5] for g in grads])
        slots = jnp.where(
            jnp.arange(n_tp)[:, None] == t, bias_rows[None, :], 0.0
        ).reshape(-1)
        packed = jnp.concatenate([vector_rows.reshape(-1), slots])
        pad = -packed.size % 1024
        packed = jnp.concatenate([packed, jnp.zeros((pad,), F32)]).reshape(-1, 128)
        packed = reduce_small(packed).reshape(-1)
        vector_rows = packed[: vector_rows.size].reshape(-1, width)
        bias_rows = lax.dynamic_slice_in_dim(
            packed, vector_rows.size + t * bias_rows.size, bias_rows.size
        )
        mine = lax.dynamic_slice_in_dim(vector_rows, s * own, own, axis=1)
        norm_part = mine[: 4 * LAYERS].reshape(LAYERS, 2, 2, own)
        out_b = mine[4 * LAYERS :].reshape(LAYERS, 1, own)
        out_b = jnp.broadcast_to(out_b, (LAYERS, 2, own))
        qkv_b = bias_rows[: LAYERS * qkv_width].reshape(LAYERS, heads, -1)
        qkv_b = lax.dynamic_slice_in_dim(qkv_b, s * qkv_bias.shape[2], qkv_bias.shape[2], axis=2)
        up_b = bias_rows[LAYERS * qkv_width :].reshape(LAYERS, up_bias.shape[1], -1)
        up_b = lax.dynamic_slice_in_dim(up_b, s * up_bias.shape[2], up_bias.shape[2], axis=2)

        rest = [g[1] for g in grads]
        grad_qkv = jnp.stack([g[0] for g in grads])
        grad_up = jnp.stack([r[:, :up_width] for r in rest])
        grad_out = jnp.stack([r[:, up_width : up_width + out_width].T for r in rest])
        grad_down = jnp.stack([r[:, up_width + out_width :].T for r in rest])
        return (
            leave(current),
            leave(grad_current),
            norm_part[:, 0],
            norm_part[:, 1],
            grad_qkv,
            qkv_b,
            grad_out,
            grad_up,
            up_b,
            grad_down,
            out_b,
        )

    return shards


def solution(mesh):
    in_specs = (
        P(("shard", "ctx"), None),
        P(("shard", "ctx"), None),
        P(("shard", "ctx")),
        P(("shard", "ctx")),
        P(None, None, "shard"),
        P(None, None, "shard"),
        P(None, "shard", "tp"),
        P(None, "tp", "shard"),
        P(None, "tp", "shard"),
        P(None, "shard", "tp"),
        P(None, "tp", "shard"),
        P(None, "tp", "shard"),
        P(None, None, "shard"),
    )
    out_specs = (
        P(("shard", "ctx"), None),
        P(("shard", "ctx"), None),
        P(None, None, "shard"),
        P(None, None, "shard"),
        P(None, "shard", "tp"),
        P(None, "tp", "shard"),
        P(None, "tp", "shard"),
        P(None, "shard", "tp"),
        P(None, "tp", "shard"),
        P(None, "tp", "shard"),
        P(None, None, "shard"),
    )
    shards = make_shards(dict(mesh.shape))
    return jax.shard_map(shards, mesh=mesh, in_specs=in_specs, out_specs=out_specs, check_vma=False)
```
